32 devices in a mesh: gx: 16 (over z, y, core), gy: 2 (over x).
Axes of the slice: x: 2, y: 2, z: 4, core: 2. Of those that a mesh axis runs over, the one named last changes fastest.
Arguments:
- planes: bfloat16 [3, 64, 128, 128], P(None, 'gx', 'gy'), may hold values from -6 to 6
- kernel: bfloat16 [3, 3, 3, 16, 128], replicated, may hold values from -0.3125 to 0.3125
- bias: float32 [128], replicated, may hold values from -4 to 4
- cotangent: bfloat16 [64, 128, 128], P('gx', 'gy'), may hold values from -6 to 6
Outputs:
- output: bfloat16 [64, 128, 128], P('gx', 'gy')
- input_grad: bfloat16 [3, 64, 128, 128], P(None, 'gx', 'gy')
- kernel_grad: float32 [3, 3, 3, 16, 128], replicated
- bias_grad: float32 [128], replicated
The draws below stay inside these ranges and needn't reach their ends.
All inputs are finite; a program needn't handle non-finite values.
Results may differ from the reference program's by a relative error of at most 0.001.
Values may be sent and summed in bfloat16 or wider, within the bound.
A program may use at most 64 MiB of HBM per device.

```python
import jax
import jax.numpy as jnp
from jax import lax

C = 128
GROUPS = 8
GW = 16
NX = 64
NY = 128


def shard_levels(rng, shape, pieces, least, largest):
    loudness = 1.0
    for position, blocks in pieces:
        heights = jax.random.uniform(jax.random.fold_in(jax.random.fold_in(rng, 6), position), (blocks,), jnp.float32, least / len(pieces), largest / len(pieces))
        loudness = loudness * jnp.repeat(jnp.exp(heights), shape[position] // blocks).reshape((-1,) + (1,) * (len(shape) - 1 - position))
    return loudness


def centred(rng, shape, spread, limit, cuts=(), dtype=jnp.bfloat16):
    result = jax.random.normal(rng, shape, jnp.float32) * spread
    if len(cuts) > 0:
        result = shard_levels(rng, shape, cuts, -0.22, 0.18) * result
    return jnp.clip(result, min=-limit, max=limit).astype(dtype)


def setup_inputs(seed: int = 0) -> dict:
    arg_keys = jax.random.split(jax.random.key(seed), 5)
    return {
        "planes": centred(arg_keys[0], (3, NX, NY, C), 1.0, 6.0, ((1, 16), (2, 2))),
        "kernel": centred(arg_keys[1], (3, 3, 3, GW, C), (27 * GW) ** -0.5, 0.3125),
        "bias": centred(arg_keys[2], (C,), 1.0, 4.0, (), jnp.float32),
        "cotangent": centred(arg_keys[3], (NX, NY, C), 1.0, 6.0, ((0, 16), (1, 2))),
    }


def reference(planes, kernel, bias, cotangent):
    inputs = planes.astype(jnp.float32)
    slope = cotangent.astype(jnp.float32)
    weights = kernel.astype(jnp.float32).reshape(3, 3, 3, GW, GROUPS, GW)
    scale = 1.0 / jnp.sqrt(jnp.float32(NX * NY))
    forward = jnp.zeros((NX, NY, GROUPS, GW), jnp.float32)
    backward = []
    kernel_rows = []
    slope_groups = slope.reshape(NX, NY, GROUPS, GW)
    for depth in range(3):
        plane = inputs[depth]
        grad_plane = jnp.zeros((NX, NY, GROUPS, GW), jnp.float32)
        for tap_x in range(3):
            for tap_y in range(3):
                moved = jnp.roll(plane, (1 - tap_x, 1 - tap_y), axis=(0, 1)).reshape(NX, NY, GROUPS, GW)
                tap_w = weights[depth, tap_x, tap_y]
                forward = forward + jnp.einsum('abgi,igo->abgo', moved, tap_w)
                back_slope = jnp.roll(slope_groups, (tap_x - 1, tap_y - 1), axis=(0, 1))
                grad_plane = grad_plane + jnp.einsum('abgo,igo->abgi', back_slope, tap_w)
                kernel_rows.append(jnp.einsum('abgi,abgo->igo', moved, slope_groups).reshape(GW, C))
        backward.append(grad_plane.reshape(NX, NY, C))
    output = (forward.reshape(NX, NY, C) + bias).astype(jnp.bfloat16)
    input_grad = jnp.stack(backward).astype(jnp.bfloat16)
    kernel_grad = jnp.stack(kernel_rows).reshape(3, 3, 3, GW, C) * scale
    bias_grad = lax.optimization_barrier(jnp.sum(slope, axis=(0, 1))) * scale
    return (output, input_grad, kernel_grad, bias_grad)
```

```python
import functools

import jax
import jax.numpy as jnp
import numpy as np
from jax import lax
from jax.experimental import pallas as pl
from jax.experimental.pallas import tpu as pltpu
from jax.sharding import PartitionSpec as P

GROUPS = 8
MESH = pl.DeviceIdType.MESH
LOW_X = 4
LOW_Y = 2
PARTS = LOW_X * LOW_Y
F32 = jnp.float32
BF16 = jnp.bfloat16


def kernel_body(
    nx, ny, scale, chunk,
    planes_hbm, kernel_hbm, bias_ref, cot_hbm,
    out_hbm, grad_hbm, sums_hbm,
    planes, taps, cot, edges, edge_halo, cot_halo, planes_halo,
    weights, weights_back, planes_t, cot_views, planes_views, out_v, grad_v,
    part, recv_a, recv_b, total,
    local_sem, halo_send, halo_recv, a_send, a_recv, b_send, b_recv, c_send, c_recv,
):
    depth, wx, wy, ch = planes.shape
    cells = wx * wy
    gw = ch // GROUPS
    gx = lax.axis_index("gx")
    gy = lax.axis_index("gy")
    nb = (nx // LOW_X) * (ny // LOW_Y)
    ia = (gx % LOW_X) * LOW_Y + gy % LOW_Y
    ib = (gx // LOW_X) * (ny // LOW_Y) + gy // LOW_Y

    def peer_a(k):
        j = (ia + k) % PARTS
        return j, ((gx // LOW_X) * LOW_X + j // LOW_Y, (gy // LOW_Y) * LOW_Y + j % LOW_Y)

    def peer_b(k):
        j = (ib + k) % nb
        high_y = ny // LOW_Y
        return ((j // high_y) * LOW_X + gx % LOW_X, (j % high_y) * LOW_Y + gy % LOW_Y)

    def near(dx, dy):
        return ((gx + dx + nx) % nx, (gy + dy + ny) % ny)

    partners = [peer_a(k)[1] for k in range(1, PARTS)] + [peer_b(k) for k in range(1, nb)]
    for dy in ((0, 1) if ny == 2 else (-1, 0, 1)):
        for dx in (-1, 0, 1):
            if (dx, dy) != (0, 0):
                partners.append(near(dx, dy))
    barrier = pltpu.get_barrier_semaphore()
    for where in partners:
        pl.semaphore_signal(barrier, inc=1, device_id=where, device_id_type=MESH)

    in_cot = pltpu.make_async_copy(cot_hbm, cot, local_sem.at[0])
    in_planes = pltpu.make_async_copy(planes_hbm, planes, local_sem.at[1])
    in_taps = pltpu.make_async_copy(kernel_hbm, taps, local_sem.at[2])
    in_cot.start()
    in_planes.start()
    in_taps.start()
    in_cot.wait()
    in_planes.wait()

    rows = [(planes, (z, x)) for z in range(depth) for x in range(wx)] + [(cot, (x,)) for x in range(wx)]
    lane_row = lax.broadcasted_iota(jnp.int32, (16, ch), 0)
    low = jnp.zeros((16, ch), F32)
    high = jnp.zeros((16, ch), F32)
    for r, (ref, at) in enumerate(rows):
        first = ref[at + (slice(0, 16),)].astype(F32)[0:1]
        last = ref[at + (slice(wy - 16, wy),)].astype(F32)[15:16]
        low = jnp.where(lane_row == r, first, low)
        high = jnp.where(lane_row == r, last, high)
    edges[0] = low.astype(BF16)
    edges[1] = high.astype(BF16)

    pl.semaphore_wait(barrier, len(partners))

    def remote(src, dst, send, recv, where):
        copy = pltpu.make_async_remote_copy(
            src_ref=src, dst_ref=dst, send_sem=send, recv_sem=recv, device_id=where, device_id_type=MESH
        )
        copy.start()
        return copy

    cot_copies = [
        remote(cot.at[0], cot_halo.at[1], halo_send.at[0], halo_recv.at[0], near(-1, 0)),
        remote(cot.at[wx - 1], cot_halo.at[0], halo_send.at[1], halo_recv.at[1], near(1, 0)),
    ]
    number = 2
    for side, dy in ((1, -1), (0, 1)):
        for dx in (-1, 0, 1):
            cot_copies.append(
                remote(edges.at[1 - side], edge_halo.at[side, 1 - dx], halo_send.at[number], halo_recv.at[number], near(dx, dy))
            )
            number += 1
    planes_copies = [
        remote(planes.at[:, 0], planes_halo.at[1], halo_send.at[8], halo_recv.at[8], near(-1, 0)),
        remote(planes.at[:, wx - 1], planes_halo.at[0], halo_send.at[9], halo_recv.at[9], near(1, 0)),
    ]

    in_taps.wait()
    row_group = lax.broadcasted_iota(jnp.int32, (ch, ch), 0) // gw
    col_group = lax.broadcasted_iota(jnp.int32, (ch, ch), 1) // gw
    mask = row_group == col_group
    mask_w = jnp.where(mask, 1.0, 0.0).astype(BF16)
    for z in range(depth):
        planes_t[z * ch : (z + 1) * ch, :] = planes[z].reshape(cells, ch).astype(F32).T.astype(BF16)
        for a in range(3):
            for b in range(3):
                tile = jnp.concatenate([taps[z, a, b]] * GROUPS, axis=0) * mask_w
                weights[z, a, b * ch : (b + 1) * ch, :] = tile
                weights_back[a, z * ch : (z + 1) * ch, (2 - b) * ch : (3 - b) * ch] = tile
    spread = jnp.sum(cot[...].reshape(cells, ch).astype(F32), axis=0, keepdims=True)
    whole_row = lax.broadcasted_iota(jnp.int32, (wy, ch), 0)

    def views(target, row, value, left, right):
        value32 = value.astype(F32)
        here = slice(row * wy, (row + 1) * wy)
        target[here, ch : 2 * ch] = value
        target[here, 0:ch] = jnp.where(whole_row == 0, left, pltpu.roll(value32, 1, 0)).astype(BF16)
        target[here, 2 * ch : 3 * ch] = jnp.where(whole_row == wy - 1, right, pltpu.roll(value32, wy - 1, 0)).astype(BF16)

    def side_of(row):
        if row == 0:
            return 0, wx - 1
        if row == wx + 1:
            return 2, 0
        return 1, row - 1

    for copy in cot_copies:
        copy.wait_recv()
    halo32 = [[edge_halo[s, o].astype(F32) for o in range(3)] for s in range(2)]
    for row in range(wx + 2):
        origin, x = side_of(row)
        value = cot_halo[0] if row == 0 else cot_halo[1] if row == wx + 1 else cot[x]
        r = depth * wx + x
        views(cot_views, row, value, halo32[0][origin][r : r + 1], halo32[1][origin][r : r + 1])

    def put(row, value):
        part[row // chunk, row % chunk : row % chunk + 8, :] = value

    for a in range(3):
        full = jnp.dot(
            planes_t[...], cot_views[(2 - a) * wy : (2 - a) * wy + cells, :], preferred_element_type=F32
        )
        for z in range(depth):
            for b in range(3):
                block = full[z * ch : (z + 1) * ch, (2 - b) * ch : (3 - b) * ch]
                block = jnp.where(mask, block, 0.0).reshape(GROUPS, gw, ch).sum(axis=0)
                start = ((z * 3 + a) * 3 + b) * gw
                put(start, block[0:8])
                put(start + 8, block[8:16])
    base = depth * 9 * gw
    put(base, jnp.broadcast_to(spread, (8, ch)))
    for row in range(base + 8, PARTS * chunk, 8):
        put(row, jnp.zeros((8, ch), F32))

    a_copies = []
    for k in range(1, PARTS):
        j, where = peer_a(k)
        a_copies.append(remote(part.at[j], recv_a.at[k - 1], a_send.at[k - 1], a_recv.at[k - 1], where))

    for copy in planes_copies:
        copy.wait_recv()
    for z in range(depth):
        for row in range(wx + 2):
            origin, x = side_of(row)
            value = planes_halo[0, z] if row == 0 else planes_halo[1, z] if row == wx + 1 else planes[z, x]
            r = z * wx + x
            views(planes_views.at[z], row, value, halo32[0][origin][r : r + 1], halo32[1][origin][r : r + 1])
    forward = jnp.zeros((cells, ch), F32)
    for z in range(depth):
        for a in range(3):
            forward = forward + jnp.dot(
                planes_views[z, a * wy : a * wy + cells, :], weights[z, a], preferred_element_type=F32
            )
    out_v[...] = (forward + bias_ref[...]).astype(BF16).reshape(wx, wy, ch)
    put_out = pltpu.make_async_copy(out_v, out_hbm, local_sem.at[3])
    put_out.start()

    for copy in a_copies:
        copy.wait_recv()
    reduced = part[ia]
    for k in range(PARTS - 1):
        reduced = reduced + recv_a[k]
    recv_b[ib] = reduced
    b_copies = []
    for k in range(1, nb):
        b_copies.append(remote(recv_b.at[ib], recv_b.at[ib], b_send.at[k - 1], b_recv.at[k - 1], peer_b(k)))

    slopes = jnp.zeros((cells, depth * ch), F32)
    for a in range(3):
        slopes = slopes + lax.dot_general(
            cot_views[(2 - a) * wy : (2 - a) * wy + cells, :],
            weights_back[a],
            (((1,), (1,)), ((), ())),
            preferred_element_type=F32,
        )
    for z in range(depth):
        grad_v[z] = slopes[:, z * ch : (z + 1) * ch].astype(BF16).reshape(wx, wy, ch)
    put_grad = pltpu.make_async_copy(grad_v, grad_hbm, local_sem.at[4])
    put_grad.start()

    for copy in b_copies:
        copy.wait_recv()
    value = recv_b[0]
    for k in range(1, nb):
        value = value + recv_b[k]
    total[...] = value * scale
    c_copies = []
    for k in range(1, PARTS):
        _, where = peer_a(k)
        c_copies.append(remote(total, sums_hbm.at[ia], c_send.at[k - 1], c_recv.at[k - 1], where))
    put_sum = pltpu.make_async_copy(total, sums_hbm.at[ia], local_sem.at[5])
    put_sum.start()

    for copy in cot_copies + planes_copies + a_copies + b_copies:
        copy.wait_send()
    put_out.wait()
    put_grad.wait()
    put_sum.wait()
    for copy in c_copies:
        copy.wait()


def shards(nx, ny, planes, kernel, bias, cotangent):
    depth, wx, wy, ch = planes.shape
    cells = wx * wy
    gw = ch // GROUPS
    nb = (nx // LOW_X) * (ny // LOW_Y)
    needed = depth * 9 * gw + 8
    chunk = -(-needed // (PARTS * 8)) * 8
    scale = np.float32(1.0) / np.sqrt(np.float32(cells * nx * ny))
    dma = pltpu.SemaphoreType.DMA
    any_space = pl.BlockSpec(memory_space=pl.ANY)
    out, grad, sums = pl.pallas_call(
        functools.partial(kernel_body, nx, ny, scale, chunk),
        out_shape=(
            jax.ShapeDtypeStruct((wx, wy, ch), BF16),
            jax.ShapeDtypeStruct((depth, wx, wy, ch), BF16),
            jax.ShapeDtypeStruct((PARTS, chunk, ch), F32),
        ),
        in_specs=[any_space, any_space, pl.BlockSpec(memory_space=pltpu.VMEM), any_space],
        out_specs=(any_space, any_space, any_space),
        scratch_shapes=[
            pltpu.VMEM((depth, wx, wy, ch), BF16),
            pltpu.VMEM((depth, 3, 3, gw, ch), BF16),
            pltpu.VMEM((wx, wy, ch), BF16),
            pltpu.VMEM((2, 16, ch), BF16),
            pltpu.VMEM((2, 3, 16, ch), BF16),
            pltpu.VMEM((2, wy, ch), BF16),
            pltpu.VMEM((2, depth, wy, ch), BF16),
            pltpu.VMEM((depth, 3, 3 * ch, ch), BF16),
            pltpu.VMEM((3, depth * ch, 3 * ch), BF16),
            pltpu.VMEM((depth * ch, cells), BF16),
            pltpu.VMEM(((wx + 2) * wy, 3 * ch), BF16),
            pltpu.VMEM((depth, (wx + 2) * wy, 3 * ch), BF16),
            pltpu.VMEM((wx, wy, ch), BF16),
            pltpu.VMEM((depth, wx, wy, ch), BF16),
            pltpu.VMEM((PARTS, chunk, ch), F32),
            pltpu.VMEM((PARTS - 1, chunk, ch), F32),
            pltpu.VMEM((nb, chunk, ch), F32),
            pltpu.VMEM((chunk, ch), F32),
            dma((6,)), dma((10,)), dma((10,)),
            dma((PARTS - 1,)), dma((PARTS - 1,)),
            dma((max(nb - 1, 1),)), dma((max(nb - 1, 1),)),
            dma((PARTS - 1,)), dma((PARTS - 1,)),
        ],
        compiler_params=pltpu.CompilerParams(
            collective_id=0, has_side_effects=True, vmem_limit_bytes=32 * 1024 * 1024
        ),
    )(planes, kernel, bias.reshape(1, ch), cotangent)
    flat = sums.reshape(PARTS * chunk, ch)
    base = depth * 9 * gw
    return out, grad, flat[:base].reshape(kernel.shape), flat[base]


def solution(mesh):
    in_specs = (P(None, "gx", "gy", None), P(), P(), P("gx", "gy", None))
    out_specs = (P("gx", "gy", None), P(None, "gx", "gy", None), P(), P())
    body = functools.partial(shards, mesh.shape["gx"], mesh.shape["gy"])
    return jax.shard_map(body, mesh=mesh, in_specs=in_specs, out_specs=out_specs, check_vma=False)
```

```python
import functools

import jax
import jax.numpy as jnp
import numpy as np
from jax import lax
from jax.experimental import pallas as pl
from jax.experimental.pallas import tpu as pltpu
from jax.sharding import PartitionSpec as P

GROUPS = 8
MESH = pl.DeviceIdType.MESH
LOW_X = 4
LOW_Y = 2
PARTS = LOW_X * LOW_Y
F32 = jnp.float32
BF16 = jnp.bfloat16


def kernel_body(
    nx, ny, scale, chunk,
    planes_hbm, kernel_hbm, bias_hbm, cot_hbm,
    out_ref, grad_ref, sums_ref,
    planes, taps, bias, cot, edges, edge_halo, cot_halo, planes_halo,
    weights, weights_back, planes_t, cot_views, planes_views,
    part, recv_a, recv_b,
    local_sem, halo_send, halo_recv, a_send, a_recv, b_send, b_recv, c_send, c_recv,
):
    depth, wx, wy, ch = planes.shape
    cells = wx * wy
    gw = ch // GROUPS
    gx = lax.axis_index("gx")
    gy = lax.axis_index("gy")
    nb = (nx // LOW_X) * (ny // LOW_Y)
    ia = (gx % LOW_X) * LOW_Y + gy % LOW_Y
    ib = (gx // LOW_X) * (ny // LOW_Y) + gy // LOW_Y

    def peer_a(k):
        j = (ia + k) % PARTS
        return j, ((gx // LOW_X) * LOW_X + j // LOW_Y, (gy // LOW_Y) * LOW_Y + j % LOW_Y)

    def peer_b(k):
        j = (ib + k) % nb
        high_y = ny // LOW_Y
        return ((j // high_y) * LOW_X + gx % LOW_X, (j % high_y) * LOW_Y + gy % LOW_Y)

    def near(dx, dy):
        return ((gx + dx + nx) % nx, (gy + dy + ny) % ny)

    partners = [peer_a(k)[1] for k in range(1, PARTS)] + [peer_b(k) for k in range(1, nb)]
    for dy in ((0, 1) if ny == 2 else (-1, 0, 1)):
        for dx in (-1, 0, 1):
            if (dx, dy) != (0, 0):
                partners.append(near(dx, dy))
    barrier = pltpu.get_barrier_semaphore()
    for where in partners:
        pl.semaphore_signal(barrier, inc=1, device_id=where, device_id_type=MESH)

    in_cot = pltpu.make_async_copy(cot_hbm, cot, local_sem.at[0])
    in_planes = pltpu.make_async_copy(planes_hbm, planes, local_sem.at[1])
    in_taps = pltpu.make_async_copy(kernel_hbm, taps, local_sem.at[2])
    in_cot.start()
    in_planes.start()
    in_taps.start()
    in_bias = pltpu.make_async_copy(bias_hbm, bias, local_sem.at[3])
    in_bias.start()
    in_cot.wait()
    in_planes.wait()

    rows = [(planes, (z, x)) for z in range(depth) for x in range(wx)] + [(cot, (x,)) for x in range(wx)]
    lane_row = lax.broadcasted_iota(jnp.int32, (16, ch), 0)
    low = jnp.zeros((16, ch), F32)
    high = jnp.zeros((16, ch), F32)
    for r, (ref, at) in enumerate(rows):
        first = ref[at + (slice(0, 16),)].astype(F32)[0:1]
        last = ref[at + (slice(wy - 16, wy),)].astype(F32)[15:16]
        low = jnp.where(lane_row == r, first, low)
        high = jnp.where(lane_row == r, last, high)
    edges[0] = low.astype(BF16)
    edges[1] = high.astype(BF16)

    pl.semaphore_wait(barrier, len(partners))

    def remote(src, dst, send, recv, where):
        copy = pltpu.make_async_remote_copy(
            src_ref=src, dst_ref=dst, send_sem=send, recv_sem=recv, device_id=where, device_id_type=MESH
        )
        copy.start()
        return copy

    cot_copies = [
        remote(cot.at[0], cot_halo.at[1], halo_send.at[0], halo_recv.at[0], near(-1, 0)),
        remote(cot.at[wx - 1], cot_halo.at[0], halo_send.at[1], halo_recv.at[1], near(1, 0)),
    ]
    number = 2
    for side, dy in ((1, -1), (0, 1)):
        for dx in (-1, 0, 1):
            cot_copies.append(
                remote(edges.at[1 - side], edge_halo.at[side, 1 - dx], halo_send.at[number], halo_recv.at[number], near(dx, dy))
            )
            number += 1
    planes_copies = [
        remote(planes.at[:, 0], planes_halo.at[1], halo_send.at[8], halo_recv.at[8], near(-1, 0)),
        remote(planes.at[:, wx - 1], planes_halo.at[0], halo_send.at[9], halo_recv.at[9], near(1, 0)),
    ]

    in_taps.wait()
    in_bias.wait()
    row_group = lax.broadcasted_iota(jnp.int32, (ch, ch), 0) // gw
    col_group = lax.broadcasted_iota(jnp.int32, (ch, ch), 1) // gw
    mask = row_group == col_group
    mask_w = jnp.where(mask, 1.0, 0.0).astype(BF16)
    for z in range(depth):
        planes_t[z * ch : (z + 1) * ch, :] = planes[z].reshape(cells, ch).astype(F32).T.astype(BF16)
        for a in range(3):
            for b in range(3):
                tile = jnp.concatenate([taps[z, a, b]] * GROUPS, axis=0) * mask_w
                weights[z, a, b * ch : (b + 1) * ch, :] = tile
                weights_back[a, z * ch : (z + 1) * ch, (2 - b) * ch : (3 - b) * ch] = tile
    spread = jnp.sum(cot[...].reshape(cells, ch).astype(F32), axis=0, keepdims=True)
    whole_row = lax.broadcasted_iota(jnp.int32, (wy, ch), 0)

    def views(target, row, value, left, right):
        value32 = value.astype(F32)
        here = slice(row * wy, (row + 1) * wy)
        target[here, ch : 2 * ch] = value
        target[here, 0:ch] = jnp.where(whole_row == 0, left, pltpu.roll(value32, 1, 0)).astype(BF16)
        target[here, 2 * ch : 3 * ch] = jnp.where(whole_row == wy - 1, right, pltpu.roll(value32, wy - 1, 0)).astype(BF16)

    def side_of(row):
        if row == 0:
            return 0, wx - 1
        if row == wx + 1:
            return 2, 0
        return 1, row - 1

    for copy in cot_copies:
        copy.wait_recv()
    halo32 = [[edge_halo[s, o].astype(F32) for o in range(3)] for s in range(2)]
    for row in range(wx + 2):
        origin, x = side_of(row)
        value = cot_halo[0] if row == 0 else cot_halo[1] if row == wx + 1 else cot[x]
        r = depth * wx + x
        views(cot_views, row, value, halo32[0][origin][r : r + 1], halo32[1][origin][r : r + 1])

    def put(row, value):
        part[row // chunk, row % chunk : row % chunk + 8, :] = value

    for a in range(3):
        full = jnp.dot(
            planes_t[...], cot_views[(2 - a) * wy : (2 - a) * wy + cells, :], preferred_element_type=F32
        )
        for z in range(depth):
            for b in range(3):
                block = full[z * ch : (z + 1) * ch, (2 - b) * ch : (3 - b) * ch]
                block = jnp.where(mask, block, 0.0).reshape(GROUPS, gw, ch).sum(axis=0)
                start = ((z * 3 + a) * 3 + b) * gw
                put(start, block[0:8])
                put(start + 8, block[8:16])
    base = depth * 9 * gw
    put(base, jnp.broadcast_to(spread, (8, ch)))
    for row in range(base + 8, PARTS * chunk, 8):
        put(row, jnp.zeros((8, ch), F32))

    a_copies = []
    for k in range(1, PARTS):
        j, where = peer_a(k)
        a_copies.append(remote(part.at[j], recv_a.at[k - 1], a_send.at[k - 1], a_recv.at[k - 1], where))

    for copy in planes_copies:
        copy.wait_recv()
    for z in range(depth):
        for row in range(wx + 2):
            origin, x = side_of(row)
            value = planes_halo[0, z] if row == 0 else planes_halo[1, z] if row == wx + 1 else planes[z, x]
            r = z * wx + x
            views(planes_views.at[z], row, value, halo32[0][origin][r : r + 1], halo32[1][origin][r : r + 1])
    forward = jnp.zeros((cells, ch), F32)
    for z in range(depth):
        for a in range(3):
            forward = forward + jnp.dot(
                planes_views[z, a * wy : a * wy + cells, :], weights[z, a], preferred_element_type=F32
            )
    out_ref[...] = (forward + bias[...]).astype(BF16).reshape(wx, wy, ch)

    for copy in a_copies:
        copy.wait_recv()
    reduced = part[ia]
    for k in range(PARTS - 1):
        reduced = reduced + recv_a[k]
    recv_b[ib] = reduced
    b_copies = []
    for k in range(1, nb):
        b_copies.append(remote(recv_b.at[ib], recv_b.at[ib], b_send.at[k - 1], b_recv.at[k - 1], peer_b(k)))

    slopes = jnp.zeros((cells, depth * ch), F32)
    for a in range(3):
        slopes = slopes + lax.dot_general(
            cot_views[(2 - a) * wy : (2 - a) * wy + cells, :],
            weights_back[a],
            (((1,), (1,)), ((), ())),
            preferred_element_type=F32,
        )
    for z in range(depth):
        grad_ref[z] = slopes[:, z * ch : (z + 1) * ch].astype(BF16).reshape(wx, wy, ch)

    for copy in b_copies:
        copy.wait_recv()
    value = recv_b[0]
    for k in range(1, nb):
        value = value + recv_b[k]
    sums_ref[ia] = value * scale
    c_copies = []
    for k in range(1, PARTS):
        _, where = peer_a(k)
        c_copies.append(remote(sums_ref.at[ia], sums_ref.at[ia], c_send.at[k - 1], c_recv.at[k - 1], where))

    for copy in cot_copies + planes_copies + a_copies + b_copies:
        copy.wait_send()
    for copy in c_copies:
        copy.wait()


def place_body(out_from, grad_from, sums, out_to, grad_to, kernel_to, bias_to, sem):
    base = kernel_to.shape[0]
    copies = [
        pltpu.make_async_copy(grad_from, grad_to, sem.at[0]),
        pltpu.make_async_copy(sums.at[0:base], kernel_to, sem.at[1]),
        pltpu.make_async_copy(out_from, out_to, sem.at[2]),
        pltpu.make_async_copy(sums.at[base : base + 1], bias_to, sem.at[3]),
    ]
    for copy in copies:
        copy.start()
    for copy in copies:
        copy.wait()


def shards(nx, ny, planes, kernel, bias, cotangent):
    depth, wx, wy, ch = planes.shape
    cells = wx * wy
    gw = ch // GROUPS
    nb = (nx // LOW_X) * (ny // LOW_Y)
    needed = depth * 9 * gw + 8
    chunk = -(-needed // (PARTS * 8)) * 8
    scale = np.float32(1.0) / np.sqrt(np.float32(cells * nx * ny))
    dma = pltpu.SemaphoreType.DMA
    vmem = pl.BlockSpec(memory_space=pltpu.VMEM)
    hbm = pl.BlockSpec(memory_space=pltpu.HBM)
    out, grad, sums = pl.pallas_call(
        functools.partial(kernel_body, nx, ny, scale, chunk),
        out_shape=(
            jax.ShapeDtypeStruct((wx, wy, ch), BF16),
            jax.ShapeDtypeStruct((depth, wx, wy, ch), BF16),
            jax.ShapeDtypeStruct((PARTS, chunk, ch), F32),
        ),
        in_specs=[hbm, hbm, hbm, hbm],
        out_specs=(vmem,) * 3,
        scratch_shapes=[
            pltpu.VMEM((depth, wx, wy, ch), BF16),
            pltpu.VMEM((depth, 3, 3, gw, ch), BF16),
            pltpu.VMEM((1, ch), F32),
            pltpu.VMEM((wx, wy, ch), BF16),
            pltpu.VMEM((2, 16, ch), BF16),
            pltpu.VMEM((2, 3, 16, ch), BF16),
            pltpu.VMEM((2, wy, ch), BF16),
            pltpu.VMEM((2, depth, wy, ch), BF16),
            pltpu.VMEM((depth, 3, 3 * ch, ch), BF16),
            pltpu.VMEM((3, depth * ch, 3 * ch), BF16),
            pltpu.VMEM((depth * ch, cells), BF16),
            pltpu.VMEM(((wx + 2) * wy, 3 * ch), BF16),
            pltpu.VMEM((depth, (wx + 2) * wy, 3 * ch), BF16),
            pltpu.VMEM((PARTS, chunk, ch), F32),
            pltpu.VMEM((PARTS - 1, chunk, ch), F32),
            pltpu.VMEM((nb, chunk, ch), F32),
            dma((4,)), dma((10,)), dma((10,)),
            dma((PARTS - 1,)), dma((PARTS - 1,)),
            dma((max(nb - 1, 1),)), dma((max(nb - 1, 1),)),
            dma((PARTS - 1,)), dma((PARTS - 1,)),
        ],
        compiler_params=pltpu.CompilerParams(
            collective_id=0, has_side_effects=True, vmem_limit_bytes=32 * 1024 * 1024
        ),
    )(*(pltpu.with_memory_space_constraint(x, pltpu.HBM) for x in (planes, kernel, bias.reshape(1, ch), cotangent)))
    base = depth * 9 * gw
    out, grad, kernel_grad, bias_grad = pl.pallas_call(
        place_body,
        out_shape=(
            jax.ShapeDtypeStruct(out.shape, BF16),
            jax.ShapeDtypeStruct(grad.shape, BF16),
            jax.ShapeDtypeStruct((base, ch), F32),
            jax.ShapeDtypeStruct((1, ch), F32),
        ),
        in_specs=[vmem] * 3,
        out_specs=(hbm, hbm, hbm, hbm),
        scratch_shapes=[dma((4,))],
    )(*(pltpu.with_memory_space_constraint(x, pltpu.VMEM) for x in (out, grad, sums.reshape(PARTS * chunk, ch))))
    return out, grad, kernel_grad.reshape(kernel.shape), bias_grad.reshape(ch)


def solution(mesh):
    in_specs = (P(None, "gx", "gy", None), P(), P(), P("gx", "gy", None))
    out_specs = (P("gx", "gy", None), P(None, "gx", "gy", None), P(), P())
    body = functools.partial(shards, mesh.shape["gx"], mesh.shape["gy"])
    return jax.shard_map(body, mesh=mesh, in_specs=in_specs, out_specs=out_specs, check_vma=False)
```

```python
import functools

import jax
import jax.numpy as jnp
import numpy as np
from jax import lax
from jax.experimental import pallas as pl
from jax.experimental.pallas import tpu as pltpu
from jax.sharding import PartitionSpec as P

GROUPS = 8
MESH = pl.DeviceIdType.MESH
LOW_X = 4
LOW_Y = 2
PARTS = LOW_X * LOW_Y
F32 = jnp.float32
BF16 = jnp.bfloat16


def kernel_body(
    nx, ny, scale, chunk,
    planes_hbm, kernel_hbm, bias_hbm, cot_hbm,
    out_ref, grad_ref, sums_ref,
    planes, taps, bias, cot, edges, edge_halo, cot_halo, planes_halo,
    weights, weights_back, planes_t, cot_views, planes_views,
    part, recv_a, recv_b,
    local_sem, halo_send, halo_recv, a_send, a_recv, b_send, b_recv, c_send, c_recv,
):
    depth, wx, wy, ch = planes.shape
    cells = wx * wy
    gw = ch // GROUPS
    gx = lax.axis_index("gx")
    gy = lax.axis_index("gy")
    nb = (nx // LOW_X) * (ny // LOW_Y)
    high_y = ny // LOW_Y
    low_gx, low_gy = lax.rem(gx, LOW_X), lax.rem(gy, LOW_Y)
    high_gx, high_gy = lax.div(gx, LOW_X), lax.div(gy, LOW_Y)
    ia = low_gx * LOW_Y + low_gy
    ib = high_gx * high_y + high_gy
    peers_a = [None]
    for k in range(1, PARTS):
        j = lax.rem(ia + k, PARTS)
        peers_a.append((j, (high_gx * LOW_X + lax.div(j, LOW_Y), high_gy * LOW_Y + lax.rem(j, LOW_Y))))
    peers_b = [None]
    for k in range(1, nb):
        j = lax.rem(ib + k, nb)
        peers_b.append((lax.div(j, high_y) * LOW_X + low_gx, lax.rem(j, high_y) * LOW_Y + low_gy))
    around_x = {-1: lax.rem(gx + nx - 1, nx), 0: gx, 1: lax.rem(gx + 1, nx)}
    around_y = {-1: lax.rem(gy + ny - 1, ny), 0: gy, 1: lax.rem(gy + 1, ny)}

    def peer_a(k):
        return peers_a[k]

    def peer_b(k):
        return peers_b[k]

    def near(dx, dy):
        return (around_x[dx], around_y[dy])

    partners = [peer_a(k)[1] for k in range(1, PARTS)] + [peer_b(k) for k in range(1, nb)]
    for dy in ((0, 1) if ny == 2 else (-1, 0, 1)):
        for dx in (-1, 0, 1):
            if (dx, dy) != (0, 0):
                partners.append(near(dx, dy))
    in_cot = pltpu.make_async_copy(cot_hbm, cot, local_sem.at[0])
    in_planes = pltpu.make_async_copy(planes_hbm, planes, local_sem.at[1])
    in_taps = pltpu.make_async_copy(kernel_hbm, taps, local_sem.at[2])
    in_cot.start()
    in_planes.start()
    in_taps.start()
    in_bias = pltpu.make_async_copy(bias_hbm, bias, local_sem.at[3])
    in_bias.start()
    barrier = pltpu.get_barrier_semaphore()
    for where in partners:
        pl.semaphore_signal(barrier, inc=1, device_id=where, device_id_type=MESH)

    in_cot.wait()
    in_planes.wait()

    rows = [(planes, (z, x)) for z in range(depth) for x in range(wx)] + [(cot, (x,)) for x in range(wx)]
    lane_row = lax.broadcasted_iota(jnp.int32, (16, ch), 0)
    low = jnp.zeros((16, ch), F32)
    high = jnp.zeros((16, ch), F32)
    for r, (ref, at) in enumerate(rows):
        first = ref[at + (slice(0, 16),)].astype(F32)[0:1]
        last = ref[at + (slice(wy - 16, wy),)].astype(F32)[15:16]
        low = jnp.where(lane_row == r, first, low)
        high = jnp.where(lane_row == r, last, high)
    edges[0] = low.astype(BF16)
    edges[1] = high.astype(BF16)

    pl.semaphore_wait(barrier, len(partners))

    def remote(src, dst, send, recv, where):
        copy = pltpu.make_async_remote_copy(
            src_ref=src, dst_ref=dst, send_sem=send, recv_sem=recv, device_id=where, device_id_type=MESH
        )
        copy.start()
        return copy

    cot_copies = [
        remote(cot.at[0], cot_halo.at[1], halo_send.at[0], halo_recv.at[0], near(-1, 0)),
        remote(cot.at[wx - 1], cot_halo.at[0], halo_send.at[1], halo_recv.at[1], near(1, 0)),
    ]
    number = 2
    for side, dy in ((1, -1), (0, 1)):
        for dx in (-1, 0, 1):
            cot_copies.append(
                remote(edges.at[1 - side], edge_halo.at[side, 1 - dx], halo_send.at[number], halo_recv.at[number], near(dx, dy))
            )
            number += 1
    planes_copies = [
        remote(planes.at[:, 0], planes_halo.at[1], halo_send.at[8], halo_recv.at[8], near(-1, 0)),
        remote(planes.at[:, wx - 1], planes_halo.at[0], halo_send.at[9], halo_recv.at[9], near(1, 0)),
    ]

    row_group = lax.broadcasted_iota(jnp.int32, (ch, ch), 0) // gw
    col_group = lax.broadcasted_iota(jnp.int32, (ch, ch), 1) // gw
    mask = row_group == col_group
    mask_w = jnp.where(mask, 1.0, 0.0).astype(BF16)
    for z in range(depth):
        planes_t[z * ch : (z + 1) * ch, :] = planes[z].reshape(cells, ch).astype(F32).T.astype(BF16)
    spread = jnp.sum(cot[...].reshape(cells, ch).astype(F32), axis=0, keepdims=True)
    whole_row = lax.broadcasted_iota(jnp.int32, (wy, ch), 0)

    def views(target, row, value, left, right):
        value32 = value.astype(F32)
        here = slice(row * wy, (row + 1) * wy)
        target[here, ch : 2 * ch] = value
        target[here, 0:ch] = jnp.where(whole_row == 0, left, pltpu.roll(value32, 1, 0)).astype(BF16)
        target[here, 2 * ch : 3 * ch] = jnp.where(whole_row == wy - 1, right, pltpu.roll(value32, wy - 1, 0)).astype(BF16)

    def side_of(row):
        if row == 0:
            return 0, wx - 1
        if row == wx + 1:
            return 2, 0
        return 1, row - 1

    for copy in cot_copies:
        copy.wait_recv()
    halo32 = [[edge_halo[s, o].astype(F32) for o in range(3)] for s in range(2)]
    for row in range(wx + 2):
        origin, x = side_of(row)
        value = cot_halo[0] if row == 0 else cot_halo[1] if row == wx + 1 else cot[x]
        r = depth * wx + x
        views(cot_views, row, value, halo32[0][origin][r : r + 1], halo32[1][origin][r : r + 1])

    def put(row, value):
        part[row // chunk, row % chunk : row % chunk + 8, :] = value

    for a in range(3):
        full = jnp.dot(
            planes_t[...], cot_views[(2 - a) * wy : (2 - a) * wy + cells, :], preferred_element_type=F32
        )
        for z in range(depth):
            for b in range(3):
                block = full[z * ch : (z + 1) * ch, (2 - b) * ch : (3 - b) * ch]
                block = jnp.where(mask, block, 0.0).reshape(GROUPS, gw, ch).sum(axis=0)
                start = ((z * 3 + a) * 3 + b) * gw
                put(start, block[0:8])
                put(start + 8, block[8:16])
    base = depth * 9 * gw
    put(base, jnp.broadcast_to(spread, (8, ch)))
    for row in range(base + 8, PARTS * chunk, 8):
        put(row, jnp.zeros((8, ch), F32))

    pieces = [slice(0, 32), slice(32, chunk)]
    a_copies = [[], []]
    for h, rows in enumerate(pieces):
        for k in range(1, PARTS):
            j, where = peer_a(k)
            a_copies[h].append(
                remote(part.at[j, rows], recv_a.at[k - 1, rows], a_send.at[h, k - 1], a_recv.at[h, k - 1], where)
            )

    in_taps.wait()
    in_bias.wait()
    for z in range(depth):
        for a in range(3):
            for b in range(3):
                tile = jnp.concatenate([taps[z, a, b]] * GROUPS, axis=0) * mask_w
                weights[z, a, b * ch : (b + 1) * ch, :] = tile
                weights_back[a, z * ch : (z + 1) * ch, (2 - b) * ch : (3 - b) * ch] = tile
    for copy in planes_copies:
        copy.wait_recv()
    for z in range(depth):
        for row in range(wx + 2):
            origin, x = side_of(row)
            value = planes_halo[0, z] if row == 0 else planes_halo[1, z] if row == wx + 1 else planes[z, x]
            r = z * wx + x
            views(planes_views.at[z], row, value, halo32[0][origin][r : r + 1], halo32[1][origin][r : r + 1])
    forward = jnp.zeros((cells, ch), F32)
    for z in range(depth):
        for a in range(3):
            forward = forward + jnp.dot(
                planes_views[z, a * wy : a * wy + cells, :], weights[z, a], preferred_element_type=F32
            )
    out_ref[...] = (forward + bias[...]).astype(BF16).reshape(wx, wy, ch)

    b_copies = [[], []]
    for h, rows in enumerate(pieces):
        for copy in a_copies[h]:
            copy.wait_recv()
        reduced = part[ia, rows]
        for k in range(PARTS - 1):
            reduced = reduced + recv_a[k, rows]
        recv_b[ib, rows] = reduced
        for k in range(1, nb):
            b_copies[h].append(
                remote(recv_b.at[ib, rows], recv_b.at[ib, rows], b_send.at[h, k - 1], b_recv.at[h, k - 1], peer_b(k))
            )

    slopes = jnp.zeros((cells, depth * ch), F32)
    for a in range(3):
        slopes = slopes + lax.dot_general(
            cot_views[(2 - a) * wy : (2 - a) * wy + cells, :],
            weights_back[a],
            (((1,), (1,)), ((), ())),
            preferred_element_type=F32,
        )
    for z in range(depth):
        grad_ref[z] = slopes[:, z * ch : (z + 1) * ch].astype(BF16).reshape(wx, wy, ch)

    c_copies = []
    for h, rows in enumerate(pieces):
        for copy in b_copies[h]:
            copy.wait_recv()
        value = recv_b[0, rows]
        for k in range(1, nb):
            value = value + recv_b[k, rows]
        sums_ref[ia, rows] = value * scale
        for k in range(1, PARTS):
            _, where = peer_a(k)
            c_copies.append(
                remote(sums_ref.at[ia, rows], sums_ref.at[ia, rows], c_send.at[h, k - 1], c_recv.at[h, k - 1], where)
            )

    for copy in cot_copies + planes_copies + sum(a_copies + b_copies, []):
        copy.wait_send()
    for copy in c_copies:
        copy.wait()


def place_body(out_from, grad_from, sums, out_to, grad_to, kernel_to, bias_to, sem):
    base = kernel_to.shape[0]
    copies = [
        pltpu.make_async_copy(grad_from, grad_to, sem.at[0]),
        pltpu.make_async_copy(sums.at[0:base], kernel_to, sem.at[1]),
        pltpu.make_async_copy(out_from, out_to, sem.at[2]),
        pltpu.make_async_copy(sums.at[base : base + 1], bias_to, sem.at[3]),
    ]
    for copy in copies:
        copy.start()
    for copy in copies:
        copy.wait()


def shards(nx, ny, planes, kernel, bias, cotangent):
    depth, wx, wy, ch = planes.shape
    cells = wx * wy
    gw = ch // GROUPS
    nb = (nx // LOW_X) * (ny // LOW_Y)
    needed = depth * 9 * gw + 8
    chunk = -(-needed // (PARTS * 8)) * 8
    scale = np.float32(1.0) / np.sqrt(np.float32(cells * nx * ny))
    dma = pltpu.SemaphoreType.DMA
    vmem = pl.BlockSpec(memory_space=pltpu.VMEM)
    hbm = pl.BlockSpec(memory_space=pltpu.HBM)
    out, grad, sums = pl.pallas_call(
        functools.partial(kernel_body, nx, ny, scale, chunk),
        out_shape=(
            jax.ShapeDtypeStruct((wx, wy, ch), BF16),
            jax.ShapeDtypeStruct((depth, wx, wy, ch), BF16),
            jax.ShapeDtypeStruct((PARTS, chunk, ch), F32),
        ),
        in_specs=[hbm, hbm, hbm, hbm],
        out_specs=(vmem,) * 3,
        scratch_shapes=[
            pltpu.VMEM((depth, wx, wy, ch), BF16),
            pltpu.VMEM((depth, 3, 3, gw, ch), BF16),
            pltpu.VMEM((1, ch), F32),
            pltpu.VMEM((wx, wy, ch), BF16),
            pltpu.VMEM((2, 16, ch), BF16),
            pltpu.VMEM((2, 3, 16, ch), BF16),
            pltpu.VMEM((2, wy, ch), BF16),
            pltpu.VMEM((2, depth, wy, ch), BF16),
            pltpu.VMEM((depth, 3, 3 * ch, ch), BF16),
            pltpu.VMEM((3, depth * ch, 3 * ch), BF16),
            pltpu.VMEM((depth * ch, cells), BF16),
            pltpu.VMEM(((wx + 2) * wy, 3 * ch), BF16),
            pltpu.VMEM((depth, (wx + 2) * wy, 3 * ch), BF16),
            pltpu.VMEM((PARTS, chunk, ch), F32),
            pltpu.VMEM((PARTS - 1, chunk, ch), F32),
            pltpu.VMEM((nb, chunk, ch), F32),
            dma((4,)), dma((10,)), dma((10,)),
            dma((2, PARTS - 1)), dma((2, PARTS - 1)),
            dma((2, max(nb - 1, 1))), dma((2, max(nb - 1, 1))),
            dma((2, PARTS - 1)), dma((2, PARTS - 1)),
        ],
        compiler_params=pltpu.CompilerParams(
            collective_id=0, has_side_effects=True, vmem_limit_bytes=32 * 1024 * 1024
        ),
    )(*(pltpu.with_memory_space_constraint(x, pltpu.HBM) for x in (planes, kernel, bias.reshape(1, ch), cotangent)))
    base = depth * 9 * gw
    out, grad, kernel_grad, bias_grad = pl.pallas_call(
        place_body,
        out_shape=(
            jax.ShapeDtypeStruct(out.shape, BF16),
            jax.ShapeDtypeStruct(grad.shape, BF16),
            jax.ShapeDtypeStruct((base, ch), F32),
            jax.ShapeDtypeStruct((1, ch), F32),
        ),
        in_specs=[vmem] * 3,
        out_specs=(hbm, hbm, hbm, hbm),
        scratch_shapes=[dma((4,))],
    )(*(pltpu.with_memory_space_constraint(x, pltpu.VMEM) for x in (out, grad, sums.reshape(PARTS * chunk, ch))))
    return out, grad, kernel_grad.reshape(kernel.shape), bias_grad.reshape(ch)


def solution(mesh):
    in_specs = (P(None, "gx", "gy", None), P(), P(), P("gx", "gy", None))
    out_specs = (P("gx", "gy", None), P(None, "gx", "gy", None), P(), P())
    body = functools.partial(shards, mesh.shape["gx"], mesh.shape["gy"])
    return jax.shard_map(body, mesh=mesh, in_specs=in_specs, out_specs=out_specs, check_vma=False)
```
